32 devices in a mesh: ens: 2 (over x), lon: 16 (over z, y, core).
Axes of the slice: x: 2, y: 2, z: 4, core: 2. Of those that a mesh axis runs over, the one named last changes fastest.
Arguments:
- state: bfloat16 [256, 4, 64, 256], P(('ens', 'lon')), parts along dimension 0, may hold values from -24 to 24
- obs_index: int32 [8192], P(('ens', 'lon')), parts along dimension 0, may hold values from 0 to 511
- obs_value: float32 [8192], P(('ens', 'lon')), parts along dimension 0, may hold values from -20 to 20
- obs_var: float32 [8192], P(('ens', 'lon')), parts along dimension 0, may hold values from 0.5 to 2
Outputs:
- analysis: bfloat16 [256, 4, 64, 256], P(('ens', 'lon')), parts along dimension 0
The draws below stay inside these ranges and needn't reach their ends.
There are 2 independent parts, one for each index of `ens`. The reference program is written for one: setup_inputs(seed, part) draws one part's arguments, and reference() takes and returns one part's arrays. A program takes and returns all parts, laid end to end along the dimension named above; each array names one. Nothing has to cross between parts.
Inputs may be any that keep to these rules, and one draw needn't show every extreme that they name: `obs_index`: a column of the device's own strip.
All inputs are finite; a program needn't handle non-finite values.
Results may differ from the reference program's by a relative error of at most 0.0029.
Values may be sent and summed in bfloat16 or wider, within the bound.
A program may use at most 128 MiB of HBM per device.

```python
import math
import jax
import jax.numpy as jnp
from jax import lax

MEM = 256
VARS = 4
REGION = 8
HALO = 4
SWEEPS = 4
LON_DEV = 8
LAT = 64
OBS_DEV = 256
NLON = 128
NOBS = 4096
N_LON = 16


def draw_state(key, part):
    base = jnp.clip(jax.random.normal(key, (NLON, VARS, LAT, MEM), jnp.float32), -6.0, 6.0)
    return base.astype(jnp.bfloat16)


def draw_obs_value(key, part):
    place = jnp.arange(NOBS) // OBS_DEV
    rise = 1.0 + 2.0 * place.astype(jnp.float32) / max(N_LON - 1, 1)
    base = jnp.clip(jax.random.normal(key, (NOBS,), jnp.float32), -6.0, 6.0)
    return base * rise


def set_ends(values, key, low, top_value):
    longest = values.shape.index(max(values.shape))
    spots = []
    for shift in (0, 1):
        where = [jax.random.randint(jax.random.fold_in(key, axis), (), 0, length) for axis, length in enumerate(values.shape)]
        where[longest] = (where[longest] + shift) % values.shape[longest]
        spots.append(tuple(where))
    return values.at[spots[0]].set(low).at[spots[1]].set(top_value)


def block_levels(rng, extent, pieces, smallest, top_value):
    loudness = 1.0
    for axis_at, shards_of in pieces:
        steps = jax.random.uniform(jax.random.fold_in(jax.random.fold_in(rng, 6), axis_at), (shards_of,), jnp.float32, smallest / len(pieces), top_value / len(pieces))
        loudness = loudness * jnp.repeat(jnp.exp(steps), extent[axis_at] // shards_of).reshape((-1,) + (1,) * (len(extent) - 1 - axis_at))
    return loudness


def setup_inputs(seed: int = 0, part: int = 0) -> dict:
    seeds = jax.random.split(jax.random.key(seed), 5)
    part_splits = jax.random.split(jax.random.fold_in(seeds[4], part), 5)
    state = draw_state(jax.random.fold_in(jax.random.fold_in(seeds[4], part), 71), part)
    obs_index = set_ends(jax.random.randint(part_splits[1], (NOBS,), 0, LON_DEV * LAT), jax.random.fold_in(part_splits[1], 1), 0, (LON_DEV * LAT) - 1).astype(jnp.int32)
    obs_value = draw_obs_value(jax.random.fold_in(jax.random.fold_in(seeds[4], part), 71), part)
    obs_var = jnp.clip(jnp.exp(math.log(2.0) - 1.3862944 * jax.random.uniform(part_splits[3], (NOBS,), jnp.float32) ** block_levels(part_splits[3], (NOBS,), ((0, 16),), -0.2, 0.2)), 0.5, 2.0)
    return {"state": state, "obs_index": obs_index, "obs_value": obs_value, "obs_var": obs_var}


EPS = 0.05


def taper():
    place = jnp.arange(REGION + 2 * HALO)
    dist = jnp.maximum(0, jnp.maximum(HALO - place, place - (HALO + REGION - 1)))
    line = 1.0 - dist.astype(jnp.float32) / (HALO + 1)
    return line[:, None] * line[None, :]


def windows(block):
    lon_len, nvar, lat_len, members = block.shape
    lon_blocks = lon_len // REGION
    lat_blocks = lat_len // REGION
    split = block.reshape(lon_blocks, REGION, nvar, lat_blocks, REGION, members)
    split = jnp.concatenate([split[:-1], split[1:]], axis=1)
    return jnp.concatenate([split[:, :, :, :-1], split[:, :, :, 1:]], axis=4)


def analyse(win, mis_win, beta):
    rho = taper()
    members = win.shape[-1]
    weighted = (win.astype(jnp.float32) * rho[None, :, None, None, :, None]).astype(jnp.bfloat16)
    weighted = lax.optimization_barrier(weighted)
    gram = jnp.einsum("apvbqm,apvbqn->abmn", weighted.astype(jnp.float32), win.astype(jnp.float32), precision=lax.Precision.HIGHEST)
    diag = jnp.diagonal(gram, axis1=2, axis2=3)
    cost = (diag[..., :, None] + diag[..., None, :] - 2.0 * gram) / (win.shape[2] * jnp.sum(rho))
    like = -0.5 * beta * jnp.einsum("apxbqm,pq->abm", mis_win, rho, precision=lax.Precision.HIGHEST)
    logw = like - jax.nn.logsumexp(like, axis=-1, keepdims=True)
    pot_g = jnp.zeros(like.shape, jnp.float32)
    pot_f = pot_g
    for sweep in range(SWEEPS):
        pot_f = EPS * logw - EPS * jax.nn.logsumexp((pot_g[..., None, :] - cost) / EPS, axis=-1)
        pot_g = -EPS * jnp.log(1.0 * members) - EPS * jax.nn.logsumexp((pot_f[..., :, None] - cost) / EPS, axis=-2)
    transport = (members * jnp.exp((pot_f[..., :, None] + pot_g[..., None, :] - cost) / EPS)).astype(jnp.bfloat16)
    own = win[:, HALO:HALO + REGION, :, :, HALO:HALO + REGION, :]
    result = jnp.einsum("apvbqi,abij->apvbqj", own.astype(jnp.float32), transport.astype(jnp.float32), precision=lax.Precision.HIGHEST)
    return result.astype(jnp.bfloat16)


def reference(state, obs_index, obs_value, obs_var):
    nlon, nvar, lat, members = state.shape
    nobs = obs_index.shape[0]
    owner = jnp.arange(nobs, dtype=jnp.int32) // OBS_DEV
    column = ((owner * LON_DEV + obs_index // LAT) * LAT + obs_index % LAT).astype(jnp.int32)
    rows = state[:, 0].reshape(nlon * lat, members)
    seen = jnp.take(rows, column, axis=0).astype(jnp.float32)
    centre = jnp.mean(seen, axis=1)
    spread = jnp.sum((seen - centre[:, None]) ** 2, axis=1) / (members - 1)
    beta = nobs / jnp.sum((obs_value - centre) ** 2 / (obs_var + spread))
    terms = (obs_value[:, None] - seen) ** 2 / obs_var[:, None]
    misfit = jax.ops.segment_sum(terms, column, num_segments=nlon * lat).reshape(nlon, 1, lat, members)
    state_pad = jnp.concatenate([state[-HALO:], state, state[:HALO]], axis=0)
    state_pad = jnp.pad(state_pad, ((0, 0), (0, 0), (HALO, HALO), (0, 0)))
    mis_pad = jnp.concatenate([misfit[-HALO:], misfit, misfit[:HALO]], axis=0)
    mis_pad = jnp.pad(mis_pad, ((0, 0), (0, 0), (HALO, HALO), (0, 0)))

    def one_column(index):
        start = (index * REGION).astype(jnp.int32)
        block = lax.dynamic_slice_in_dim(state_pad, start, REGION + 2 * HALO, 0)
        mblock = lax.dynamic_slice_in_dim(mis_pad, start, REGION + 2 * HALO, 0)
        out = analyse(windows(block), windows(mblock), beta)
        return out.reshape(REGION, nvar, lat, members)

    result = lax.map(one_column, jnp.arange(nlon // REGION, dtype=jnp.int32))
    return result.reshape(nlon, nvar, lat, members)
```

```python
import functools
import jax
import jax.numpy as jnp
from jax import lax
from jax.experimental import pallas as pl
from jax.experimental.pallas import tpu as pltpu
from jax.sharding import PartitionSpec as P

REGION = 8
HALO = 4
SWEEPS = 4
EPS = 0.05
TILE = 16
MESH = pl.DeviceIdType.MESH


def line(place):
    dist = jnp.maximum(0.0, jnp.maximum(HALO - place, place - (HALO + REGION - 1)))
    return jnp.maximum(0.0, 1.0 - dist / (HALO + 1))


def rho_sum():
    return sum(
        1.0 - max(0, HALO - p, p - (HALO + REGION - 1)) / (HALO + 1) for p in range(REGION + 2 * HALO)
    ) ** 2


def row_lse(pot_g, cost_ref):
    members = cost_ref.shape[0]
    parts = []
    for start in range(0, members, 64):
        arg = pot_g - cost_ref[start : start + 64, :]
        top = jnp.max(arg, axis=1, keepdims=True)
        parts.append(top + jnp.log(jnp.sum(jnp.exp(arg - top), axis=1, keepdims=True)))
    return jnp.concatenate(parts, axis=0)


def column_lse(pot_f, cost_ref):
    arg = pot_f - cost_ref[...]
    top = jnp.max(arg, axis=0, keepdims=True)
    return top + jnp.log(jnp.sum(jnp.exp(arg - top), axis=0, keepdims=True))


def kernel(
    count, state_ref, index_ref, value_ref, var_ref, out_ref,
    buf, win, wgt, own, cost, logw, parts, like_out, like_in, out_buf,
    own_sem, halo_send, halo_recv, like_send, like_recv, part_send, part_recv, out_sem,
):
    lon_dev, nvar, lat, members = state_ref.shape
    span = REGION + 2 * HALO
    chunks = lat // TILE
    regions = lat // REGION
    me = lax.axis_index("lon")
    right, left = lax.rem(me + 1, count), lax.rem(me + count - 1, count)

    barrier = pltpu.get_barrier_semaphore()

    @pl.loop(1, count)
    def _(hop):
        pl.semaphore_signal(
            barrier, inc=1, device_id={"lon": lax.rem(me + hop, count)}, device_id_type=MESH
        )

    own_copy = pltpu.make_async_copy(
        state_ref, buf.at[pl.ds(HALO, lon_dev), :, pl.ds(TILE, lat), :], own_sem
    )
    own_copy.start()
    blank = jnp.zeros((span, nvar, TILE, members), jnp.bfloat16)
    buf[:, :, 0:TILE, :] = blank
    buf[:, :, TILE + lat : 2 * TILE + lat, :] = blank
    pl.semaphore_wait(barrier, count - 1)

    def halo_copy(side, chunk):
        return pltpu.make_async_remote_copy(
            src_ref=state_ref.at[
                pl.ds(lon_dev - HALO if side == 0 else 0, HALO), :, pl.ds(chunk * TILE, TILE), :
            ],
            dst_ref=buf.at[
                pl.ds(0 if side == 0 else HALO + lon_dev, HALO), :, pl.ds(TILE + chunk * TILE, TILE), :
            ],
            send_sem=halo_send.at[side, chunk],
            recv_sem=halo_recv.at[side, chunk],
            device_id={"lon": right if side == 0 else left},
            device_id_type=MESH,
        )

    for chunk in range(min(2, chunks)):
        for side in range(2):
            halo_copy(side, chunk).start()
    own_copy.wait()

    index = index_ref[...]
    value = value_ref[...]
    var = var_ref[...]
    nobs = index.shape[1]
    rows = buf[HALO : HALO + lon_dev, 0, TILE : TILE + lat, :].reshape(lon_dev * lat, members)
    onehot = (lax.broadcasted_iota(jnp.int32, (lon_dev * lat, nobs), 0) == index).astype(jnp.float32)
    seen = lax.dot_general(
        rows, onehot.astype(jnp.bfloat16), (((0,), (0,)), ((), ())), preferred_element_type=jnp.float32
    )
    centre = jnp.sum(seen, axis=0, keepdims=True) / members
    spread = jnp.sum((seen - centre) ** 2, axis=0, keepdims=True) / (members - 1)
    partial_value = jnp.sum((value - centre) ** 2 / (var + spread), axis=1, keepdims=True)
    parts[0] = jnp.broadcast_to(partial_value, (8, 128))

    lon_of = jnp.zeros(index.shape, jnp.int32)
    for lon in range(1, lon_dev):
        lon_of = lon_of + (index >= lon * lat).astype(jnp.int32)
    lat_of = (index - lon_of * lat).astype(jnp.float32)
    lon_of = lon_of.astype(jnp.float32)
    region = lax.broadcasted_iota(jnp.int32, (regions, nobs), 0).astype(jnp.float32)
    weight = line(lat_of - region * REGION + HALO) / var
    weights = jnp.concatenate(
        [
            weight,
            weight * line(lon_of - lon_dev + HALO),
            weight * line(lon_of + lon_dev + HALO),
        ],
        axis=0,
    )
    square = (value - seen) ** 2
    like = lax.dot_general(
        weights, square, (((1,), (1,)), ((), ())),
        precision=lax.Precision.HIGHEST, preferred_element_type=jnp.float32,
    )
    like_out[0] = like[regions : 2 * regions]
    like_out[1] = like[2 * regions : 3 * regions]
    like_own = like[0:regions]

    def part_copy(hop):
        return pltpu.make_async_remote_copy(
            src_ref=parts.at[0],
            dst_ref=parts.at[hop],
            send_sem=part_send.at[hop],
            recv_sem=part_recv.at[hop],
            device_id={"lon": lax.rem(me + hop, count)},
            device_id_type=MESH,
        )

    def like_copy(side):
        return pltpu.make_async_remote_copy(
            src_ref=like_out.at[side],
            dst_ref=like_in.at[side],
            send_sem=like_send.at[side],
            recv_sem=like_recv.at[side],
            device_id={"lon": right if side == 0 else left},
            device_id_type=MESH,
        )

    @pl.loop(1, count)
    def _(hop):
        part_copy(hop).start()

    for side in range(2):
        like_copy(side).start()
    for chunk in range(2, chunks):
        for side in range(2):
            halo_copy(side, chunk).start()

    def pair_build(step, lons):
        base = pl.multiple_of(step * TILE, TILE)
        place = lax.broadcasted_iota(jnp.int32, (span, members), 0).astype(jnp.float32)
        taper = line(place)
        for lon in lons:
            rho = taper * (1.0 - max(0, HALO - lon, lon - (HALO + REGION - 1)) / (HALO + 1))
            for variable in range(nvar):
                x = buf[lon, variable, pl.ds(base, 3 * TILE), :].astype(jnp.float32)
                y = x[TILE - HALO : TILE + 2 * REGION + HALO]
                for a in range(2):
                    w = y[a * REGION : a * REGION + span]
                    win[a, lon, variable] = w.astype(jnp.bfloat16)
                    wgt[a, lon, variable] = (w * rho).astype(jnp.bfloat16)
                    if HALO <= lon < HALO + REGION:
                        own[a, lon - HALO, variable] = x[
                            TILE + a * REGION : TILE + (a + 1) * REGION
                        ]

    scale = 1.0 / (nvar * rho_sum() * EPS)

    def gram_cost(a):
        depth = span * nvar * span
        gram = lax.dot_general(
            wgt[a].reshape(depth, members), win[a].reshape(depth, members),
            (((0,), (0,)), ((), ())), preferred_element_type=jnp.float32,
        )
        shape = (members, members)
        eye = lax.broadcasted_iota(jnp.int32, shape, 0) == lax.broadcasted_iota(jnp.int32, shape, 1)
        only = jnp.where(eye, gram, 0.0)
        diag_row = jnp.sum(only, axis=0, keepdims=True)
        diag_col = jnp.sum(only, axis=1, keepdims=True)
        cost[a] = (diag_col + diag_row - 2.0 * gram) * scale

    def body(step, carry):
        pair_build(step, range(HALO, HALO + lon_dev))
        for chunk in range(chunks):
            @pl.when(step == max(chunk - 1, 0))
            def _():
                for side in range(2):
                    halo_copy(side, chunk).wait_recv()

        pair_build(step, list(range(HALO)) + list(range(HALO + lon_dev, span)))
        for a in range(2):
            gram_cost(a)

        @pl.when(step == 0)
        def _():
            @pl.loop(1, count)
            def _(hop):
                part_copy(hop).wait_recv()

            total = lax.fori_loop(
                1, count, lambda hop, acc: acc + parts[hop], parts[0]
            )[0:1, 0:1]
            factor = -0.5 * (count * nobs) / total
            for side in range(2):
                like_copy(side).wait_recv()
            every = factor * (like_own_ref(like_in) + like_in[0] + like_in[1])
            top = jnp.max(every, axis=1, keepdims=True)
            every = every - (top + jnp.log(jnp.sum(jnp.exp(every - top), axis=1, keepdims=True)))
            turned = jnp.transpose(every)
            for r in range(regions):
                logw[r] = jnp.broadcast_to(turned[:, r : r + 1], (members, 128))

        pot_f = [None, None]
        pot_g = [jnp.zeros((1, members), jnp.float32)] * 2
        for sweep in range(SWEEPS):
            for a in range(2):
                pot_f[a] = logw[2 * step + a][:, 0:1] - row_lse(pot_g[a], cost.at[a])
            for a in range(2):
                pot_g[a] = -jnp.log(jnp.float32(members)) - column_lse(pot_f[a], cost.at[a])
        results = []
        for a in range(2):
            transport = (members * jnp.exp(pot_f[a] + pot_g[a] - cost[a])).astype(jnp.bfloat16)
            lhs = own[a].reshape(lon_dev * nvar * REGION, members).astype(jnp.bfloat16)
            res = jnp.dot(lhs, transport, preferred_element_type=jnp.float32)
            results.append(res.reshape(lon_dev, nvar, REGION, members))
        out_buf[step] = jnp.concatenate(results, axis=2).astype(jnp.bfloat16)
        out_copy(step).start()
        return carry

    def like_own_ref(_):
        return like_in[2]

    def out_copy(step):
        return pltpu.make_async_copy(
            out_buf.at[step],
            out_ref.at[:, :, pl.ds(pl.multiple_of(step * TILE, TILE), TILE), :],
            out_sem.at[step],
        )

    like_in[2] = like_own
    lax.fori_loop(0, chunks, body, 0)

    for chunk in range(chunks):
        for side in range(2):
            halo_copy(side, chunk).wait_send()
    for side in range(2):
        like_copy(side).wait_send()

    @pl.loop(1, count)
    def _(hop):
        part_copy(hop).wait_send()

    @pl.loop(0, chunks)
    def _(step):
        out_copy(step).wait()


def on_device(state, obs_index, obs_value, obs_var):
    lon_dev, nvar, lat, members = state.shape
    nobs = obs_index.shape[0]
    count = lax.axis_size("lon")
    span = REGION + 2 * HALO
    chunks = lat // TILE
    regions = lat // REGION
    dma = pltpu.SemaphoreType.DMA
    vmem = pl.BlockSpec(memory_space=pltpu.VMEM)
    hbm = pl.BlockSpec(memory_space=pl.ANY)
    return pl.pallas_call(
        functools.partial(kernel, count),
        out_shape=jax.ShapeDtypeStruct(state.shape, state.dtype),
        in_specs=[hbm, vmem, vmem, vmem],
        out_specs=hbm,
        scratch_shapes=[
            pltpu.VMEM((span, nvar, lat + 2 * TILE, members), jnp.bfloat16),
            pltpu.VMEM((2, span, nvar, span, members), jnp.bfloat16),
            pltpu.VMEM((2, span, nvar, span, members), jnp.bfloat16),
            pltpu.VMEM((2, lon_dev, nvar, REGION, members), jnp.float32),
            pltpu.VMEM((2, members, members), jnp.float32),
            pltpu.VMEM((regions, members, 128), jnp.float32),
            pltpu.VMEM((count, 8, 128), jnp.float32),
            pltpu.VMEM((2, regions, members), jnp.float32),
            pltpu.VMEM((3, regions, members), jnp.float32),
            pltpu.VMEM((chunks, lon_dev, nvar, TILE, members), jnp.bfloat16),
            dma, dma((2, chunks)), dma((2, chunks)), dma((2,)), dma((2,)),
            dma((count,)), dma((count,)), dma((chunks,)),
        ],
        compiler_params=pltpu.CompilerParams(
            collective_id=0, has_side_effects=True, vmem_limit_bytes=48 << 20
        ),
        name="analysis",
    )(
        state,
        obs_index.reshape(1, nobs),
        obs_value.reshape(1, nobs),
        obs_var.reshape(1, nobs),
    )


def solution(mesh):
    return jax.shard_map(
        on_device,
        mesh=mesh,
        in_specs=(
            P(("ens", "lon"), None, None, None),
            P(("ens", "lon")),
            P(("ens", "lon")),
            P(("ens", "lon")),
        ),
        out_specs=P(("ens", "lon"), None, None, None),
        check_vma=False,
    )
```

```python
import functools
import math
import jax
import jax.numpy as jnp
from jax import lax
from jax.experimental import pallas as pl
from jax.experimental.pallas import tpu as pltpu
from jax.sharding import PartitionSpec as P

REGION = 8
HALO = 4
SWEEPS = 4
EPS = 0.05
TILE = 16
LANES = 128
STRIP = 64
MESH = pl.DeviceIdType.MESH


def line(place):
    dist = jnp.maximum(0.0, jnp.maximum(HALO - place, place - (HALO + REGION - 1)))
    return jnp.maximum(0.0, 1.0 - dist / (HALO + 1))


def rho_sum():
    return sum(
        1.0 - max(0, HALO - p, p - (HALO + REGION - 1)) / (HALO + 1) for p in range(REGION + 2 * HALO)
    ) ** 2


def log2(x):
    return jnp.log(x) * (1.0 / math.log(2.0))


def row_lse(pot_g, cost_ref):
    members = cost_ref.shape[0]
    parts = []
    for start in range(0, members, STRIP):
        args = [
            pot_g[:, at : at + LANES] - cost_ref[start : start + STRIP, at : at + LANES]
            for at in range(0, members, LANES)
        ]
        top = jnp.max(functools.reduce(jnp.maximum, args), axis=1, keepdims=True)
        top = jnp.broadcast_to(top, (STRIP, LANES))
        total = functools.reduce(jnp.add, [jnp.exp2(arg - top) for arg in args])
        total = jnp.broadcast_to(jnp.sum(total, axis=1, keepdims=True), (STRIP, LANES))
        parts.append(top + log2(total))
    return jnp.concatenate(parts, axis=0)


def column_lse(pot_f, cost_ref):
    members = cost_ref.shape[0]
    parts = []
    for at in range(0, members, LANES):
        arg = pot_f - cost_ref[:, at : at + LANES]
        top = jnp.max(arg, axis=0, keepdims=True)
        parts.append(top + log2(jnp.sum(jnp.exp2(arg - top), axis=0, keepdims=True)))
    return jnp.concatenate(parts, axis=1)


def kernel(
    count, state_ref, index_hbm, value_hbm, var_hbm, out_ref,
    index_ref, value_ref, var_ref,    buf, win, wgt, own, cost, logw, parts, like_out, like_in, out_buf,
    own_sem, obs_sem, halo_send, halo_recv, like_send, like_recv, part_send, part_recv, out_sem,
):
    lon_dev, nvar, lat, members = state_ref.shape
    span = REGION + 2 * HALO
    chunks = lat // TILE
    regions = lat // REGION
    me = lax.axis_index("lon")
    right, left = lax.rem(me + 1, count), lax.rem(me + count - 1, count)

    barrier = pltpu.get_barrier_semaphore()

    @pl.loop(1, count)
    def _(hop):
        pl.semaphore_signal(
            barrier, inc=1, device_id={"lon": lax.rem(me + hop, count)}, device_id_type=MESH
        )

    own_copy = pltpu.make_async_copy(
        state_ref, buf.at[pl.ds(HALO, lon_dev), :, pl.ds(TILE, lat), :], own_sem
    )
    own_copy.start()
    obs_copies = [
        pltpu.make_async_copy(src, dst, obs_sem.at[at])
        for at, (src, dst) in enumerate(
            ((index_hbm, index_ref), (value_hbm, value_ref), (var_hbm, var_ref))
        )
    ]
    for copy in obs_copies:
        copy.start()
    blank = jnp.zeros((span, nvar, TILE, members), jnp.bfloat16)
    buf[:, :, 0:TILE, :] = blank
    buf[:, :, TILE + lat : 2 * TILE + lat, :] = blank

    def halo_copy(side, chunk):
        return pltpu.make_async_remote_copy(
            src_ref=state_ref.at[
                pl.ds(lon_dev - HALO if side == 0 else 0, HALO), :, pl.ds(chunk * TILE, TILE), :
            ],
            dst_ref=buf.at[
                pl.ds(0 if side == 0 else HALO + lon_dev, HALO), :, pl.ds(TILE + chunk * TILE, TILE), :
            ],
            send_sem=halo_send.at[side, chunk],
            recv_sem=halo_recv.at[side, chunk],
            device_id={"lon": right if side == 0 else left},
            device_id_type=MESH,
        )

    own_copy.wait()
    for copy in obs_copies:
        copy.wait()

    index = index_ref[...]
    value = value_ref[...]
    var = var_ref[...]
    nobs = index.shape[1]
    rows = buf[HALO : HALO + lon_dev, 0, TILE : TILE + lat, :].reshape(lon_dev * lat, members)
    onehot = (lax.broadcasted_iota(jnp.int32, (lon_dev * lat, nobs), 0) == index).astype(jnp.float32)
    seen = lax.dot_general(
        rows, onehot.astype(jnp.bfloat16), (((0,), (0,)), ((), ())), preferred_element_type=jnp.float32
    )
    centre = jnp.sum(seen, axis=0, keepdims=True) / members
    spread = jnp.sum((seen - centre) ** 2, axis=0, keepdims=True) / (members - 1)
    partial_value = jnp.sum((value - centre) ** 2 / (var + spread), axis=1, keepdims=True)
    parts[0] = jnp.broadcast_to(partial_value, (8, 128))

    def part_copy(hop):
        return pltpu.make_async_remote_copy(
            src_ref=parts.at[0],
            dst_ref=parts.at[hop],
            send_sem=part_send.at[hop],
            recv_sem=part_recv.at[hop],
            device_id={"lon": lax.rem(me + hop, count)},
            device_id_type=MESH,
        )

    pl.semaphore_wait(barrier, count - 1)

    @pl.loop(1, count)
    def _(hop):
        part_copy(hop).start()

    for chunk in range(min(2, chunks)):
        for side in range(2):
            halo_copy(side, chunk).start()

    lon_of = jnp.zeros(index.shape, jnp.int32)
    for lon in range(1, lon_dev):
        lon_of = lon_of + (index >= lon * lat).astype(jnp.int32)
    lat_of = (index - lon_of * lat).astype(jnp.float32)
    lon_of = lon_of.astype(jnp.float32)
    region = lax.broadcasted_iota(jnp.int32, (regions, nobs), 0).astype(jnp.float32)
    weight = line(lat_of - region * REGION + HALO) / var
    weights = jnp.concatenate(
        [
            weight,
            weight * line(lon_of - lon_dev + HALO),
            weight * line(lon_of + lon_dev + HALO),
        ],
        axis=0,
    )
    square = (value - seen) ** 2
    like = lax.dot_general(
        weights, square, (((1,), (1,)), ((), ())),
        precision=lax.Precision.HIGHEST, preferred_element_type=jnp.float32,
    )
    like_out[0] = like[regions : 2 * regions]
    like_out[1] = like[2 * regions : 3 * regions]
    like_own = like[0:regions]

    def like_copy(side):
        return pltpu.make_async_remote_copy(
            src_ref=like_out.at[side],
            dst_ref=like_in.at[side],
            send_sem=like_send.at[side],
            recv_sem=like_recv.at[side],
            device_id={"lon": right if side == 0 else left},
            device_id_type=MESH,
        )

    for side in range(2):
        like_copy(side).start()
    for chunk in range(2, chunks):
        for side in range(2):
            halo_copy(side, chunk).start()

    def pair_build(step, lons):
        base = pl.multiple_of(step * TILE, TILE)
        place = lax.broadcasted_iota(jnp.int32, (span, members), 0).astype(jnp.float32)
        taper = line(place)
        for lon in lons:
            rho = taper * (1.0 - max(0, HALO - lon, lon - (HALO + REGION - 1)) / (HALO + 1))
            for variable in range(nvar):
                x = buf[lon, variable, pl.ds(base, 3 * TILE), :].astype(jnp.float32)
                y = x[TILE - HALO : TILE + 2 * REGION + HALO]
                for a in range(2):
                    w = y[a * REGION : a * REGION + span]
                    win[a, lon, variable] = w.astype(jnp.bfloat16)
                    wgt[a, lon, variable] = (w * rho).astype(jnp.bfloat16)
                    if HALO <= lon < HALO + REGION:
                        own[a, lon - HALO, variable] = x[
                            TILE + a * REGION : TILE + (a + 1) * REGION
                        ]

    scale = 1.0 / (nvar * rho_sum() * EPS * math.log(2.0))

    def gram_cost(a):
        depth = span * nvar * span
        gram = lax.dot_general(
            wgt[a].reshape(depth, members), win[a].reshape(depth, members),
            (((0,), (0,)), ((), ())), preferred_element_type=jnp.float32,
        )
        shape = (members, members)
        eye = lax.broadcasted_iota(jnp.int32, shape, 0) == lax.broadcasted_iota(jnp.int32, shape, 1)
        only = jnp.where(eye, gram, 0.0)
        diag_row = jnp.sum(only, axis=0, keepdims=True)
        diag_col = jnp.sum(only, axis=1, keepdims=True)
        cost[a] = (diag_col + diag_row - 2.0 * gram) * scale

    def body(step, carry):
        pair_build(step, range(HALO, HALO + lon_dev))
        for chunk in range(chunks):
            @pl.when(step == max(chunk - 1, 0))
            def _():
                for side in range(2):
                    halo_copy(side, chunk).wait_recv()

        pair_build(step, list(range(HALO)) + list(range(HALO + lon_dev, span)))
        for a in range(2):
            gram_cost(a)
        first = [row_lse(jnp.zeros((1, members), jnp.float32), cost.at[a]) for a in range(2)]

        @pl.when(step == 0)
        def _():
            @pl.loop(1, count)
            def _(hop):
                part_copy(hop).wait_recv()

            total = lax.fori_loop(
                1, count, lambda hop, acc: acc + parts[hop], parts[0]
            )[0:1, 0:1]
            factor = (-0.5 * count * nobs / math.log(2.0)) / total
            for side in range(2):
                like_copy(side).wait_recv()
            every = factor * (like_own_ref(like_in) + like_in[0] + like_in[1])
            top = jnp.max(every, axis=1, keepdims=True)
            every = every - (top + log2(jnp.sum(jnp.exp2(every - top), axis=1, keepdims=True)))
            turned = jnp.transpose(every)
            for r in range(regions):
                logw[r] = jnp.broadcast_to(turned[:, r : r + 1], (members, 128))

        pot_f = [logw[2 * step + a] - first[a] for a in range(2)]
        pot_g = [None, None]
        for sweep in range(SWEEPS):
            for a in range(2):
                if sweep > 0:
                    pot_f[a] = logw[2 * step + a] - row_lse(pot_g[a], cost.at[a])
            for a in range(2):
                pot_g[a] = -math.log2(members) - column_lse(pot_f[a], cost.at[a])
        results = []
        for a in range(2):
            shifted = pot_g[a] + math.log2(members)
            transport = jnp.concatenate(
                [
                    jnp.exp2(pot_f[a] + shifted[:, at : at + LANES] - cost[a, :, at : at + LANES])
                    for at in range(0, members, LANES)
                ],
                axis=1,
            ).astype(jnp.bfloat16)
            lhs = own[a].reshape(lon_dev * nvar * REGION, members).astype(jnp.bfloat16)
            res = jnp.dot(lhs, transport, preferred_element_type=jnp.float32)
            results.append(res.reshape(lon_dev, nvar, REGION, members))
        out_buf[step] = jnp.concatenate(results, axis=2).astype(jnp.bfloat16)
        out_copy(step).start()
        return carry

    def like_own_ref(_):
        return like_in[2]

    def out_copy(step):
        return pltpu.make_async_copy(
            out_buf.at[step],
            out_ref.at[:, :, pl.ds(pl.multiple_of(step * TILE, TILE), TILE), :],
            out_sem.at[step],
        )

    like_in[2] = like_own
    lax.fori_loop(0, chunks, body, 0)

    for chunk in range(chunks):
        for side in range(2):
            halo_copy(side, chunk).wait_send()
    for side in range(2):
        like_copy(side).wait_send()

    @pl.loop(1, count)
    def _(hop):
        part_copy(hop).wait_send()

    @pl.loop(0, chunks)
    def _(step):
        out_copy(step).wait()


def on_device(state, obs_index, obs_value, obs_var):
    lon_dev, nvar, lat, members = state.shape
    nobs = obs_index.shape[0]
    count = lax.axis_size("lon")
    span = REGION + 2 * HALO
    chunks = lat // TILE
    regions = lat // REGION
    dma = pltpu.SemaphoreType.DMA
    hbm = pl.BlockSpec(memory_space=pl.ANY)
    pinned = pl.BlockSpec(memory_space=pltpu.HBM)
    return pl.pallas_call(
        functools.partial(kernel, count),
        out_shape=jax.ShapeDtypeStruct(state.shape, state.dtype),
        in_specs=[pinned] * 4,
        out_specs=hbm,
        scratch_shapes=[
            pltpu.VMEM((1, nobs), jnp.int32),
            pltpu.VMEM((1, nobs), jnp.float32),
            pltpu.VMEM((1, nobs), jnp.float32),
            pltpu.VMEM((span, nvar, lat + 2 * TILE, members), jnp.bfloat16),
            pltpu.VMEM((2, span, nvar, span, members), jnp.bfloat16),
            pltpu.VMEM((2, span, nvar, span, members), jnp.bfloat16),
            pltpu.VMEM((2, lon_dev, nvar, REGION, members), jnp.float32),
            pltpu.VMEM((2, members, members), jnp.float32),
            pltpu.VMEM((regions, members, 128), jnp.float32),
            pltpu.VMEM((count, 8, 128), jnp.float32),
            pltpu.VMEM((2, regions, members), jnp.float32),
            pltpu.VMEM((3, regions, members), jnp.float32),
            pltpu.VMEM((chunks, lon_dev, nvar, TILE, members), jnp.bfloat16),
            dma, dma((3,)), dma((2, chunks)), dma((2, chunks)), dma((2,)), dma((2,)),
            dma((count,)), dma((count,)), dma((chunks,)),
        ],
        compiler_params=pltpu.CompilerParams(
            collective_id=0, has_side_effects=True, vmem_limit_bytes=48 << 20
        ),
        name="analysis",
    )(
        *[pltpu.with_memory_space_constraint(x, pltpu.HBM) for x in (state, obs_index.reshape(1, nobs), obs_value.reshape(1, nobs), obs_var.reshape(1, nobs))],
    )


def solution(mesh):
    return jax.shard_map(
        on_device,
        mesh=mesh,
        in_specs=(
            P(("ens", "lon"), None, None, None),
            P(("ens", "lon")),
            P(("ens", "lon")),
            P(("ens", "lon")),
        ),
        out_specs=P(("ens", "lon"), None, None, None),
        check_vma=False,
    )
```
